32 devices in a mesh: replica: 8 (over z, y), tp: 4 (over x, core).
Axes of the slice: x: 2, y: 2, z: 4, core: 2. Of those that a mesh axis runs over, the one named last changes fastest.
Arguments:
- hidden: bfloat16 [96, 4, 8192], P('replica', None, 'tp'), may hold values from -6 to 6
- norm_gain: float32 [8192], replicated, may hold values from 0.5 to 1.5
- w_query: float32 [8192, 4096], P(('replica', 'tp')), may hold values from -0.0625 to 0.0625
- w_key: float32 [8192, 512], P(('replica', 'tp')), may hold values from -0.0625 to 0.0625
- w_value: float32 [8192, 512], P(('replica', 'tp')), may hold values from -0.0625 to 0.0625
- bias_query: float32 [4096], P('tp'), may hold values from -3 to 3
- bias_key: float32 [512], P('tp'), may hold values from -3 to 3
- bias_value: float32 [512], P('tp'), may hold values from -3 to 3
- key_pages: bfloat16 [512, 4, 128, 128], P(('replica', 'tp')), may hold values from -256 to 256
- value_pages: bfloat16 [512, 4, 128, 128], P(('replica', 'tp')), may hold values from -6 to 6
- kv_lengths: int32 [96], P(('replica', 'tp')), may hold values from 1 to 1024, as said below
- page_table: int32 [96, 8], P(('replica', 'tp')), may hold values from 0 to 15, as said below
Outputs:
- attended: bfloat16 [96, 4, 4096], P(('replica', 'tp'))
The draws below stay inside these ranges and needn't reach their ends.
Inputs may be any that keep to these rules, and one draw needn't show every extreme that they name: `kv_lengths`: on every device, one row has exactly 1024 cached tokens. `page_table`: page ids are local to the pool of 16 pages of the device that holds the row. The first ceil(kv_lengths / 128) entries of a row name its pages in order; no page serves two of those entries on one device; later entries are arbitrary pages of the pool.
All inputs are finite; a program needn't handle non-finite values.
Results may differ from the reference program's by a relative error of at most 0.04.
Values may be sent and summed in bfloat16 or wider, within the bound.
No kernel may reach another device: no remote copies, remote signals or barrier semaphores. Data moves between devices by JAX's collectives and lax.ppermute only.
A program may use at most 128 MiB of HBM per device.

```python
import jax
import jax.numpy as jnp
from jax import lax

D = 8192
HD = 128
HQ = 32
KVH = 4
STEPS = 4
PAGE = 128
MOSTP = 8
ROWS_DEV = 3
PAGES_DEV = 16
ROWS = 96
NPAGES = 512


def layout_device(key):
    keys = jax.random.split(key, 4)
    raw = jax.random.randint(keys[0], (ROWS_DEV,), 1, MOSTP + 1)
    chosen = jax.random.randint(keys[1], (), 0, ROWS_DEV)
    index = jnp.arange(ROWS_DEV, dtype=jnp.int32)
    longest = index == chosen

    def settle(used, item):
        value, is_long, place = item
        later = ROWS_DEV - 1 - place - (chosen > place).astype(jnp.int32)
        room = PAGES_DEV - MOSTP - used - later
        amount = jnp.where(is_long, MOSTP, jnp.minimum(value, room))
        return (used + jnp.where(is_long, 0, amount), amount)
    _, counts = lax.scan(settle, jnp.int32(0), (raw, longest, index))
    trims = jax.random.randint(keys[2], (ROWS_DEV,), 0, PAGE)
    trims = jnp.where(longest, 0, trims)
    lengths = counts * PAGE - trims
    order = jax.random.permutation(keys[3], PAGES_DEV).astype(jnp.int32)
    starts = jnp.cumsum(counts) - counts
    slots = (starts[:, None] + jnp.arange(MOSTP, dtype=jnp.int32)[None, :]) % PAGES_DEV
    table = order[slots]
    return (lengths.astype(jnp.int32), table.astype(jnp.int32))


def layout_all(key):
    base = jax.random.fold_in(key, 17)
    devices = ROWS // ROWS_DEV
    keys = jax.vmap(lambda d: jax.random.fold_in(base, d))(jnp.arange(devices))
    lengths, tables = jax.vmap(layout_device)(keys)
    return (lengths.reshape(ROWS), tables.reshape(ROWS, MOSTP))


def draw_kv_lengths(key, part):
    return layout_all(key)[0]


def draw_page_table(key, part):
    return layout_all(key)[1]


def draw_key_pages(key, part):
    first = jax.random.fold_in(jax.random.fold_in(key, 5), 0)
    base = jax.random.normal(first, (NPAGES, KVH, PAGE, HD), jnp.float32)
    base = jnp.clip(base, -6.0, 6.0)
    return base.astype(jnp.bfloat16)


def block_scale(rng, extent, cuts, smallest, largest):
    gain, own = 1.0, jax.random.fold_in(rng, 6)
    for position, blocks in cuts:
        heights = jnp.exp(jax.random.uniform(jax.random.fold_in(own, position), (blocks,), jnp.float32, smallest / len(cuts), largest / len(cuts)))
        gain = gain * jnp.repeat(heights, extent[position] // blocks).reshape([-1 if axis == position else 1 for axis in range(len(extent))])
    return gain


def gaussian(rng, shape, scale, most, cuts=(), held_as=jnp.bfloat16):
    array = jax.random.normal(rng, shape, jnp.float32) * scale
    if len(cuts) > 0:
        array = block_scale(rng, shape, cuts, -0.22, 0.18) * array
    return jnp.clip(array, min=-most, max=most).astype(held_as)


def setup_inputs(seed: int = 0) -> dict:
    streams_of = jax.random.split(jax.random.key(seed), 13)
    hidden = gaussian(streams_of[0], (ROWS, STEPS, D), 1.0, 6.0, ((0, 8), (2, 4)))
    norm_gain = jnp.clip(1.0 + 0.1 * jax.random.normal(streams_of[1], (D,), jnp.float32), 0.5, 1.5)
    w_query = gaussian(streams_of[2], (D, HQ * HD), D ** -0.5, 0.0625, ((0, 32),), jnp.float32)
    w_key = gaussian(streams_of[3], (D, KVH * HD), D ** -0.5, 0.0625, ((0, 32),), jnp.float32)
    w_value = gaussian(streams_of[4], (D, KVH * HD), D ** -0.5, 0.0625, ((0, 32),), jnp.float32)
    bias_query = gaussian(streams_of[5], (HQ * HD,), 0.5, 3.0, ((0, 4),), jnp.float32)
    bias_key = gaussian(streams_of[6], (KVH * HD,), 0.5, 3.0, ((0, 4),), jnp.float32)
    bias_value = gaussian(streams_of[7], (KVH * HD,), 0.5, 3.0, ((0, 4),), jnp.float32)
    key_pages = draw_key_pages(jax.random.fold_in(streams_of[12], 71), 0)
    value_pages = gaussian(streams_of[9], (NPAGES, KVH, PAGE, HD), 1.0, 6.0, ((0, 32),))
    kv_lengths = draw_kv_lengths(jax.random.fold_in(streams_of[12], 71), 0)
    page_table = draw_page_table(jax.random.fold_in(streams_of[12], 71), 0)
    return {"hidden": hidden, "norm_gain": norm_gain, "w_query": w_query, "w_key": w_key, "w_value": w_value, "bias_query": bias_query, "bias_key": bias_key, "bias_value": bias_value, "key_pages": key_pages, "value_pages": value_pages, "kv_lengths": kv_lengths, "page_table": page_table}


EPS = 1e-06
THETA = 1000000.0

def rotate(values, positions):
    half = values.shape[-1] // 2
    freq = THETA ** (-(jnp.arange(half, dtype=jnp.float32) * 2.0 / values.shape[-1]))
    angle = positions.astype(jnp.float32)[..., None] * freq
    angle = jnp.concatenate([angle, angle], -1)[:, :, None, :]
    turned = jnp.concatenate([-values[..., half:], values[..., :half]], -1)
    return values * jnp.cos(angle) + turned * jnp.sin(angle)

def reference(hidden, norm_gain, w_query, w_key, w_value, bias_query, bias_key, bias_value, key_pages, value_pages, kv_lengths, page_table):
    count, steps, width = hidden.shape
    wide = hidden.astype(jnp.float32)
    power = lax.optimization_barrier(jnp.mean(wide * wide, axis=2, keepdims=True))
    normed = (wide * lax.rsqrt(power + EPS) * norm_gain).astype(jnp.bfloat16).reshape(count * steps, width)

    def project(weight, bias):
        out = jnp.dot(normed, weight.astype(jnp.bfloat16), preferred_element_type=jnp.float32) + bias
        return out.astype(jnp.bfloat16)
    query = project(w_query, bias_query).reshape(count, steps, HQ, HD)
    key_new = project(w_key, bias_key).reshape(count, steps, KVH, HD)
    value_new = project(w_value, bias_value).reshape(count, steps, KVH, HD)
    positions = kv_lengths[:, None] + jnp.arange(steps, dtype=jnp.int32)[None, :]
    query_rot = rotate(query.astype(jnp.float32), positions).astype(jnp.bfloat16)
    key_rot = rotate(key_new.astype(jnp.float32), positions).astype(jnp.bfloat16)
    group = HQ // KVH
    scale = 1.0 / HD ** 0.5
    causal = jnp.arange(steps)[None, :] <= jnp.arange(steps)[:, None]

    def one_row(item):
        index, q_row, k_row, v_row, length, table = item
        device = index // ROWS_DEV
        ids = (device * PAGES_DEV + table).astype(jnp.int32)
        keys = key_pages[ids].astype(jnp.float32)
        vals = value_pages[ids].astype(jnp.float32)
        q5 = q_row.astype(jnp.float32).reshape(steps, KVH, group, HD)
        cache = jnp.einsum('tkgd,mknd->tkgmn', q5, keys) * scale
        spot = jnp.arange(MOSTP)[:, None] * PAGE + jnp.arange(PAGE)[None, :]
        live = (spot < length)[None, None, None]
        cache = jnp.where(live, cache, -1e+30)
        fresh = jnp.einsum('tkgd,skd->tkgs', q5, k_row.astype(jnp.float32)) * scale
        fresh = jnp.where(causal[:, None, None, :], fresh, -1e+30)
        top = jnp.maximum(lax.optimization_barrier(jnp.max(cache, axis=(3, 4))), lax.optimization_barrier(jnp.max(fresh, axis=3)))
        e_cache = jnp.where(live, jnp.exp(cache - top[..., None, None]), 0.0)
        e_fresh = jnp.where(causal[:, None, None, :], jnp.exp(fresh - top[..., None]), 0.0)
        total = lax.optimization_barrier(jnp.sum(e_cache, axis=(3, 4))) + lax.optimization_barrier(jnp.sum(e_fresh, axis=3))
        w_cache = (e_cache / total[..., None, None]).astype(jnp.bfloat16).astype(jnp.float32)
        w_fresh = (e_fresh / total[..., None]).astype(jnp.bfloat16).astype(jnp.float32)
        out = jnp.einsum('tkgmn,mknd->tkgd', w_cache, vals)
        out = out + jnp.einsum('tkgs,skd->tkgd', w_fresh, v_row.astype(jnp.float32))
        return out.reshape(steps, HQ * HD).astype(jnp.bfloat16)
    rows_index = jnp.arange(count, dtype=jnp.int32)
    return lax.map(one_row, (rows_index, query_rot, key_rot, value_new, kv_lengths, page_table))
```

```python
import jax
import jax.numpy as jnp
from jax import lax
from jax.sharding import PartitionSpec as P

HD = 128
HQ = 32
KVH = 4
PAGE = 128
MOSTP = 8
EPS = 1e-06
THETA = 1000000.0
AXES = ("replica", "tp")
BF = jnp.bfloat16
F32 = jnp.float32


def rotate(values, positions):
    half = values.shape[-1] // 2
    freq = THETA ** (-(jnp.arange(half, dtype=jnp.float32) * 2.0 / values.shape[-1]))
    angle = positions.astype(jnp.float32)[..., None] * freq
    angle = jnp.concatenate([angle, angle], -1)[:, :, None, :]
    turned = jnp.concatenate([-values[..., half:], values[..., :half]], -1)
    return values * jnp.cos(angle) + turned * jnp.sin(angle)


def attend(query, key_new, value_new, key_pages, value_pages, kv_lengths, page_table):
    rows, steps = query.shape[:2]
    positions = kv_lengths[:, None] + jnp.arange(steps, dtype=jnp.int32)[None, :]
    query_rot = rotate(query.astype(jnp.float32), positions).astype(jnp.bfloat16)
    key_rot = rotate(key_new.astype(jnp.float32), positions).astype(jnp.bfloat16)
    group = HQ // KVH
    scale = 1.0 / HD**0.5
    q_heads = query_rot.reshape(rows, steps, KVH, group, HD)
    keys = jnp.take(key_pages, page_table, axis=0)
    vals = jnp.take(value_pages, page_table, axis=0)
    cache = (
        jnp.einsum("rtkgd,rmknd->rtkgmn", q_heads, keys, preferred_element_type=jnp.float32) * scale
    )
    spot = jnp.arange(MOSTP)[:, None] * PAGE + jnp.arange(PAGE)[None, :]
    live = (spot[None] < kv_lengths[:, None, None])[:, None, None, None]
    cache = jnp.where(live, cache, -1e30)
    causal = jnp.arange(steps)[None, :] <= jnp.arange(steps)[:, None]
    fresh = (
        jnp.einsum("rtkgd,rskd->rtkgs", q_heads, key_rot, preferred_element_type=jnp.float32)
        * scale
    )
    fresh = jnp.where(causal[None, :, None, None, :], fresh, -1e30)
    top = jnp.maximum(jnp.max(cache, axis=(4, 5)), jnp.max(fresh, axis=4))
    e_cache = jnp.where(live, jnp.exp(cache - top[..., None, None]), 0.0)
    e_fresh = jnp.where(causal[None, :, None, None, :], jnp.exp(fresh - top[..., None]), 0.0)
    total = jnp.sum(e_cache, axis=(4, 5)) + jnp.sum(e_fresh, axis=4)
    w_cache = (e_cache / total[..., None, None]).astype(jnp.bfloat16)
    w_fresh = (e_fresh / total[..., None]).astype(jnp.bfloat16)
    out = jnp.einsum("rtkgmn,rmknd->rtkgd", w_cache, vals, preferred_element_type=jnp.float32)
    out = out + jnp.einsum(
        "rtkgs,rskd->rtkgd", w_fresh, value_new, preferred_element_type=jnp.float32
    )
    return out.reshape(rows, steps, HQ * HD).astype(jnp.bfloat16)


def weights_plan(hidden, norm_gain, w_query, w_key, w_value, bias_query, bias_key, bias_value,
                 key_pages, value_pages, kv_lengths, page_table):
    shards = tuple(w.astype(BF) for w in (w_query, w_key, w_value))
    whole = lax.all_gather(hidden, "tp", axis=2, tiled=True)
    count, steps, width = whole.shape
    wide = whole.astype(F32)
    power = jnp.mean(wide * wide, axis=2, keepdims=True)
    normed = (wide * lax.rsqrt(power + EPS) * norm_gain).astype(BF).reshape(count * steps, width)
    made = []
    for shard, bias in zip(shards, (bias_query, bias_key, bias_value)):
        local = lax.all_to_all(shard, "tp", split_axis=1, concat_axis=0, tiled=True)
        piece = lax.all_gather(local, "replica", axis=0, tiled=True)
        total = jnp.dot(normed, piece, preferred_element_type=F32) + bias
        out = total.astype(BF).reshape(count, steps, -1)
        made.append(lax.all_to_all(out, "tp", split_axis=0, concat_axis=2, tiled=True))
    rows = made[0].shape[0]
    query = made[0].reshape(rows, steps, HQ, HD)
    key_new = made[1].reshape(rows, steps, KVH, HD)
    value_new = made[2].reshape(rows, steps, KVH, HD)
    return attend(query, key_new, value_new, key_pages, value_pages, kv_lengths, page_table)


def sums_plan(R, T, hidden, norm_gain, w_query, w_key, w_value, bias_query, bias_key, bias_value,
              key_pages, value_pages, kv_lengths, page_table):
    ri, ti = lax.axis_index("replica"), lax.axis_index("tp")
    me = ri * T + ti
    y, z, c, x = ri % 2, ri // 2, ti % 2, ti // 2
    Z = R // 2
    count, steps, _ = hidden.shape
    kw = w_query.shape[0]
    D = norm_gain.shape[0]
    rows = count // T
    own = rows * steps
    G = KVH // 2
    qw = HQ // KVH * HD
    gw = qw + 2 * HD

    def perm(f):
        pairs = []
        for i in range(R * T):
            r, t = divmod(i, T)
            zz, yy, xx, cc = f(r // 2, r % 2, t // 2, t % 2)
            pairs.append((i, (zz * 2 + yy) * T + xx * 2 + cc))
        return pairs

    to_core = perm(lambda z, y, x, c: (z, y, x, 1 - c))
    to_x = perm(lambda z, y, x, c: (z, y, 1 - x, c))
    to_y = perm(lambda z, y, x, c: (z, 1 - y, x, c))

    def send(a, pairs):
        return lax.ppermute(a, AXES, pairs)

    pick = lambda a, i, axis=0: lax.dynamic_index_in_dim(a, i, axis, keepdims=False)

    got = []
    for k in range(R):
        part = lax.dynamic_slice_in_dim(hidden, (ri ^ k) * kw, kw, 2)
        pairs = [(r * T + t, t * R + (r ^ k)) for r in range(R) for t in range(T)]
        got.append(send(part, pairs))
    j = me % R
    acts = jnp.take(jnp.stack(got), j ^ jnp.arange(R), axis=0)
    acts = acts.reshape(Z, 2, 2, 2 * own, kw).transpose(1, 2, 0, 3, 4).reshape(2, 2, Z * 2 * own, kw)
    acts_sib = send(acts, to_core)

    gain = lax.dynamic_slice_in_dim(norm_gain, me * kw, kw)[:, None]

    def columns(cc, g):
        h = cc + 2 * g
        parts = [
            lax.dynamic_slice_in_dim(w_query, h * qw, qw, 1),
            lax.dynamic_slice_in_dim(w_key, h * HD, HD, 1),
            lax.dynamic_slice_in_dim(w_value, h * HD, HD, 1),
        ]
        return (jnp.concatenate(parts, 1) * gain).astype(BF)

    w_own = [columns(c, g) for g in range(G)]
    w_sib = [send(columns(1 - c, g), to_core) for g in range(G)]

    wide = hidden.astype(F32)
    power = jnp.sum(wide * wide, axis=2).reshape(T, own)
    bias = jnp.concatenate([bias_query, bias_key, bias_value])
    biases = [bias]
    squares = pick(power, ti)
    for k in range(1, T):
        msg = jnp.concatenate([bias, pick(power, ti ^ k)])
        pairs = [(r * T + t, r * T + (t ^ k)) for r in range(R) for t in range(T)]
        msg = send(msg, pairs)
        biases.append(msg[: bias.shape[0]])
        squares = squares + msg[bias.shape[0] :]
    bias_all = jnp.take(jnp.stack(biases), ti ^ jnp.arange(T), axis=0)
    row_scale = lax.rsqrt(squares / D + EPS)

    def dot(g):
        f = lambda a, w: jnp.einsum("yxmk,kn->yxmn", a, w, preferred_element_type=F32)
        return f(acts, w_own[g]) + f(acts_sib, w_sib[g])

    done = []
    for g in range(G):
        part = dot(g)
        first, second = ((x, 1, to_x), (y, 0, to_y)) if g % 2 == 0 else ((y, 0, to_y), (x, 0, to_x))
        i, axis, pairs = first
        part = pick(part, i, axis) + send(pick(part, 1 - i, axis).astype(BF), pairs).astype(F32)
        i, axis, pairs = second
        part = pick(part, i, axis) + send(pick(part, 1 - i, axis).astype(BF), pairs).astype(F32)
        part = part.reshape(Z, 2 * own, gw)
        total = pick(part, z)
        for k in range(1, Z):
            pairs = perm(lambda z, y, x, c: (z ^ k, y, x, c))
            total = total + send(pick(part, z ^ k).astype(BF), pairs).astype(F32)
        done.append(total.reshape(2, own, gw))
    done = jnp.stack(done)
    mine = pick(done, c, 1)
    other = send(pick(done, 1 - c, 1), to_core)
    low, high = jnp.where(c == 0, mine, other), jnp.where(c == 0, other, mine)
    full = jnp.stack([low, high], 1).reshape(KVH, own, gw)
    full = full * row_scale[None, :, None] + bias_all[:, None, :]
    full = full.astype(BF).reshape(KVH, rows, steps, gw)
    query = full[..., :qw].reshape(KVH, rows, steps, HQ // KVH, HD).transpose(1, 2, 0, 3, 4)
    query = query.reshape(rows, steps, HQ, HD)
    key_new = full[..., qw : qw + HD].transpose(1, 2, 0, 3)
    value_new = full[..., qw + HD :].transpose(1, 2, 0, 3)
    return attend(query, key_new, value_new, key_pages, value_pages, kv_lengths, page_table)


def solution(mesh):
    R, T = mesh.shape["replica"], mesh.shape["tp"]

    def on_device(hidden, norm_gain, *rest):
        m = hidden.shape[0] * hidden.shape[1] * R
        few_rows = m * T < norm_gain.shape[0]
        two_ways = T == KVH and R & (R - 1) == 0 and R > T
        if few_rows and two_ways:
            return sums_plan(R, T, hidden, norm_gain, *rest)
        return weights_plan(hidden, norm_gain, *rest)

    split = ("replica", "tp")
    in_specs = (
        P("replica", None, "tp"), P(), P(split, None), P(split, None), P(split, None),
        P("tp"), P("tp"), P("tp"),
        P(split, None, None, None), P(split, None, None, None), P(split), P(split, None),
    )
    return jax.shard_map(
        on_device, mesh=mesh, in_specs=in_specs, out_specs=P(split, None, None), check_vma=False
    )
```

```python
import jax
import jax.numpy as jnp
from jax import lax
from jax.sharding import PartitionSpec as P

HD = 128
HQ = 32
KVH = 4
PAGE = 128
MOSTP = 8
EPS = 1e-06
THETA = 1000000.0
AXES = ("replica", "tp")
BF = jnp.bfloat16
F32 = jnp.float32


def rotate(values, positions):
    half = values.shape[-1] // 2
    freq = THETA ** (-(jnp.arange(half, dtype=jnp.float32) * 2.0 / values.shape[-1]))
    angle = positions.astype(jnp.float32)[..., None] * freq
    angle = jnp.concatenate([angle, angle], -1)[:, :, None, :]
    turned = jnp.concatenate([-values[..., half:], values[..., :half]], -1)
    return values * jnp.cos(angle) + turned * jnp.sin(angle)


def attend(query, key_new, value_new, key_pages, value_pages, kv_lengths, page_table):
    rows, steps = query.shape[:2]
    positions = kv_lengths[:, None] + jnp.arange(steps, dtype=jnp.int32)[None, :]
    query_rot = rotate(query.astype(jnp.float32), positions).astype(jnp.bfloat16)
    key_rot = rotate(key_new.astype(jnp.float32), positions).astype(jnp.bfloat16)
    group = HQ // KVH
    scale = 1.0 / HD**0.5
    q_heads = query_rot.reshape(rows, steps, KVH, group, HD)
    keys = jnp.take(key_pages, page_table, axis=0)
    vals = jnp.take(value_pages, page_table, axis=0)
    cache = (
        jnp.einsum("rtkgd,rmknd->rtkgmn", q_heads, keys, preferred_element_type=jnp.float32) * scale
    )
    spot = jnp.arange(MOSTP)[:, None] * PAGE + jnp.arange(PAGE)[None, :]
    live = (spot[None] < kv_lengths[:, None, None])[:, None, None, None]
    cache = jnp.where(live, cache, -1e30)
    causal = jnp.arange(steps)[None, :] <= jnp.arange(steps)[:, None]
    fresh = (
        jnp.einsum("rtkgd,rskd->rtkgs", q_heads, key_rot, preferred_element_type=jnp.float32)
        * scale
    )
    fresh = jnp.where(causal[None, :, None, None, :], fresh, -1e30)
    top = jnp.maximum(jnp.max(cache, axis=(4, 5)), jnp.max(fresh, axis=4))
    e_cache = jnp.where(live, jnp.exp(cache - top[..., None, None]), 0.0)
    e_fresh = jnp.where(causal[None, :, None, None, :], jnp.exp(fresh - top[..., None]), 0.0)
    total = jnp.sum(e_cache, axis=(4, 5)) + jnp.sum(e_fresh, axis=4)
    w_cache = (e_cache / total[..., None, None]).astype(jnp.bfloat16)
    w_fresh = (e_fresh / total[..., None]).astype(jnp.bfloat16)
    out = jnp.einsum("rtkgmn,rmknd->rtkgd", w_cache, vals, preferred_element_type=jnp.float32)
    out = out + jnp.einsum(
        "rtkgs,rskd->rtkgd", w_fresh, value_new, preferred_element_type=jnp.float32
    )
    return out.reshape(rows, steps, HQ * HD).astype(jnp.bfloat16)


def weights_plan(hidden, norm_gain, w_query, w_key, w_value, bias_query, bias_key, bias_value,
                 key_pages, value_pages, kv_lengths, page_table):
    shards = tuple(w.astype(BF) for w in (w_query, w_key, w_value))
    whole = lax.all_gather(hidden, "tp", axis=2, tiled=True)
    count, steps, width = whole.shape
    wide = whole.astype(F32)
    power = jnp.mean(wide * wide, axis=2, keepdims=True)
    normed = (wide * lax.rsqrt(power + EPS) * norm_gain).astype(BF).reshape(count * steps, width)
    made = []
    for shard, bias in zip(shards, (bias_query, bias_key, bias_value)):
        local = lax.all_to_all(shard, "tp", split_axis=1, concat_axis=0, tiled=True)
        piece = lax.all_gather(local, "replica", axis=0, tiled=True)
        total = jnp.dot(normed, piece, preferred_element_type=F32) + bias
        out = total.astype(BF).reshape(count, steps, -1)
        made.append(lax.all_to_all(out, "tp", split_axis=0, concat_axis=2, tiled=True))
    rows = made[0].shape[0]
    query = made[0].reshape(rows, steps, HQ, HD)
    key_new = made[1].reshape(rows, steps, KVH, HD)
    value_new = made[2].reshape(rows, steps, KVH, HD)
    return attend(query, key_new, value_new, key_pages, value_pages, kv_lengths, page_table)


def sums_plan(R, T, hidden, norm_gain, w_query, w_key, w_value, bias_query, bias_key, bias_value,
              key_pages, value_pages, kv_lengths, page_table):
    ri, ti = lax.axis_index("replica"), lax.axis_index("tp")
    me = ri * T + ti
    y, z, c, x = ri % 2, ri // 2, ti % 2, ti // 2
    Z = R // 2
    count, steps, _ = hidden.shape
    kw = w_query.shape[0]
    D = norm_gain.shape[0]
    rows = count // T
    own = rows * steps
    G = KVH // 2
    qw = HQ // KVH * HD
    gw = qw + 2 * HD

    def perm(f):
        pairs = []
        for i in range(R * T):
            r, t = divmod(i, T)
            zz, yy, xx, cc = f(r // 2, r % 2, t // 2, t % 2)
            pairs.append((i, (zz * 2 + yy) * T + xx * 2 + cc))
        return pairs

    to_core = perm(lambda z, y, x, c: (z, y, x, 1 - c))
    to_x = perm(lambda z, y, x, c: (z, y, 1 - x, c))
    to_y = perm(lambda z, y, x, c: (z, 1 - y, x, c))

    def send(a, pairs):
        return lax.ppermute(a, AXES, pairs)

    pick = lambda a, i, axis=0: lax.dynamic_index_in_dim(a, i, axis, keepdims=False)

    def both(i, mine, other):
        return jnp.stack([jnp.where(i == 0, mine, other), jnp.where(i == 0, other, mine)])

    zh, zl = z // 2, z % 2
    acts = hidden.reshape(T * own, 2, 2, 2, kw).transpose(1, 2, 3, 0, 4)
    acts = send(acts, perm(lambda z, y, x, c: (z // 2 * 2 + c, y, x, z % 2)))
    acts = both(x, pick(acts, x, 1), send(pick(acts, 1 - x, 1), to_x))
    acts = both(y, pick(acts, y, 1), send(pick(acts, 1 - y, 1), to_y))
    to_far = perm(lambda z, y, x, c: (z ^ 2, y, x, c))
    acts = both(zh, pick(acts, zh, 1), send(pick(acts, 1 - zh, 1), to_far))
    acts = both(c, acts, send(acts, to_core))
    acts_own, acts_sib = pick(acts, c, 3), pick(acts, 1 - c, 3)

    gain = lax.dynamic_slice_in_dim(norm_gain, me * kw, kw)[:, None]

    def columns(cc, g):
        h = cc + 2 * g
        parts = [
            lax.dynamic_slice_in_dim(w_query, h * qw, qw, 1),
            lax.dynamic_slice_in_dim(w_key, h * HD, HD, 1),
            lax.dynamic_slice_in_dim(w_value, h * HD, HD, 1),
        ]
        return (jnp.concatenate(parts, 1) * gain).astype(BF)

    w_own = [columns(c, g) for g in range(G)]
    w_sib = [send(columns(1 - c, g), to_core) for g in range(G)]

    wide = hidden.astype(F32)
    power = jnp.sum(wide * wide, axis=2).reshape(T * own)
    bias = jnp.concatenate([bias_query, bias_key, bias_value])
    there = send(jnp.concatenate([bias, power]), to_x)
    biases = both(x, bias, there[:gw])
    power = power + there[gw:]

    def dot(g):
        f = lambda a, w: jnp.einsum("abymk,kn->abymn", a, w, preferred_element_type=F32)
        out = f(acts_own, w_own[g]) + f(acts_sib, w_sib[g])
        return out.reshape(2, 2, 2, 2, 2 * own, gw)

    done = []
    for g in range(G):
        part = dot(g)
        for i, axis, pairs in ((x, 3, to_x), (y, 2, to_y))[:: 1 if g % 2 == 0 else -1]:
            there = send(pick(part, 1 - i, axis).astype(BF), pairs)
            part = jnp.expand_dims(pick(part, i, axis) + there.astype(F32), axis)
        part = part.reshape(2, 2, 2 * own, gw)
        at = lambda z: pick(pick(part, z % 2), z // 2)
        total = at(z)
        for k in range(1, Z):
            pairs = perm(lambda z, y, x, c: (z ^ k, y, x, c))
            total = total + send(at(z ^ k).astype(BF), pairs).astype(F32)
        done.append(total.reshape(2, own, gw))
    done = jnp.stack(done)
    mine, other = pick(done, c, 1), pick(done, 1 - c, 1)
    low = jnp.pad(power, (0, G * gw - T * own)).reshape(G, 1, gw)
    other = send(jnp.concatenate([other, biases[:, None], low], 1), to_core)
    full = both(c, mine, other[:, :own]).transpose(1, 0, 2, 3).reshape(KVH, own, gw)
    bias_all = both(c, biases, other[:, own]).transpose(1, 0, 2).reshape(KVH, gw)
    power = power + other[:, own + 1].reshape(-1)[: T * own]
    row_scale = lax.rsqrt(pick(power.reshape(T, own), ti) / D + EPS)
    full = full * row_scale[None, :, None] + bias_all[:, None, :]
    full = full.astype(BF).reshape(KVH, rows, steps, gw)
    query = full[..., :qw].reshape(KVH, rows, steps, HQ // KVH, HD).transpose(1, 2, 0, 3, 4)
    query = query.reshape(rows, steps, HQ, HD)
    key_new = full[..., qw : qw + HD].transpose(1, 2, 0, 3)
    value_new = full[..., qw + HD :].transpose(1, 2, 0, 3)
    return attend(query, key_new, value_new, key_pages, value_pages, kv_lengths, page_table)


def solution(mesh):
    R, T = mesh.shape["replica"], mesh.shape["tp"]

    def on_device(hidden, norm_gain, *rest):
        m = hidden.shape[0] * hidden.shape[1] * R
        few_rows = m * T < norm_gain.shape[0]
        two_ways = T == KVH and R == 2 * T
        if few_rows and two_ways:
            return sums_plan(R, T, hidden, norm_gain, *rest)
        return weights_plan(hidden, norm_gain, *rest)

    split = ("replica", "tp")
    in_specs = (
        P("replica", None, "tp"), P(), P(split, None), P(split, None), P(split, None),
        P("tp"), P("tp"), P("tp"),
        P(split, None, None, None), P(split, None, None, None), P(split), P(split, None),
    )
    return jax.shard_map(
        on_device, mesh=mesh, in_specs=in_specs, out_specs=P(split, None, None), check_vma=False
    )
```

```python
import functools

import jax
import jax.numpy as jnp
from jax import lax
from jax.experimental import pallas as pl
from jax.experimental.pallas import tpu as pltpu
from jax.sharding import PartitionSpec as P

HD = 128
HQ = 32
KVH = 4
PAGE = 128
MOSTP = 8
EPS = 1e-06
THETA = 1000000.0
AXES = ("replica", "tp")
BF = jnp.bfloat16
F32 = jnp.float32


def rotate(values, positions):
    half = values.shape[-1] // 2
    freq = THETA ** (-(jnp.arange(half, dtype=jnp.float32) * 2.0 / values.shape[-1]))
    angle = positions.astype(jnp.float32)[..., None] * freq
    angle = jnp.concatenate([angle, angle], -1)[:, :, None, :]
    turned = jnp.concatenate([-values[..., half:], values[..., :half]], -1)
    return values * jnp.cos(angle) + turned * jnp.sin(angle)


def attend(query, key_new, value_new, key_pages, value_pages, kv_lengths, page_table):
    rows, steps = query.shape[:2]
    positions = kv_lengths[:, None] + jnp.arange(steps, dtype=jnp.int32)[None, :]
    query_rot = rotate(query.astype(jnp.float32), positions).astype(jnp.bfloat16)
    key_rot = rotate(key_new.astype(jnp.float32), positions).astype(jnp.bfloat16)
    group = HQ // KVH
    scale = 1.0 / HD**0.5
    q_heads = query_rot.reshape(rows, steps, KVH, group, HD)
    keys = jnp.take(key_pages, page_table, axis=0)
    vals = jnp.take(value_pages, page_table, axis=0)
    cache = (
        jnp.einsum("rtkgd,rmknd->rtkgmn", q_heads, keys, preferred_element_type=jnp.float32) * scale
    )
    spot = jnp.arange(MOSTP)[:, None] * PAGE + jnp.arange(PAGE)[None, :]
    live = (spot[None] < kv_lengths[:, None, None])[:, None, None, None]
    cache = jnp.where(live, cache, -1e30)
    causal = jnp.arange(steps)[None, :] <= jnp.arange(steps)[:, None]
    fresh = (
        jnp.einsum("rtkgd,rskd->rtkgs", q_heads, key_rot, preferred_element_type=jnp.float32)
        * scale
    )
    fresh = jnp.where(causal[None, :, None, None, :], fresh, -1e30)
    top = jnp.maximum(jnp.max(cache, axis=(4, 5)), jnp.max(fresh, axis=4))
    e_cache = jnp.where(live, jnp.exp(cache - top[..., None, None]), 0.0)
    e_fresh = jnp.where(causal[None, :, None, None, :], jnp.exp(fresh - top[..., None]), 0.0)
    total = jnp.sum(e_cache, axis=(4, 5)) + jnp.sum(e_fresh, axis=4)
    w_cache = (e_cache / total[..., None, None]).astype(jnp.bfloat16)
    w_fresh = (e_fresh / total[..., None]).astype(jnp.bfloat16)
    out = jnp.einsum("rtkgmn,rmknd->rtkgd", w_cache, vals, preferred_element_type=jnp.float32)
    out = out + jnp.einsum(
        "rtkgs,rskd->rtkgd", w_fresh, value_new, preferred_element_type=jnp.float32
    )
    return out.reshape(rows, steps, HQ * HD).astype(jnp.bfloat16)


def attend_kernel(heads, len_ref, tab_ref, core_ref, mine, other, scale, bias, cos, sin, keys, vals,
                  out, q32, qb, kf, vf, score, top, low, acc):
    slots = keys.shape[0]
    rows, steps = out.shape[:2]
    most = tab_ref.shape[1]
    own = rows * steps
    group = mine.shape[2] // HD - 2
    lanes = group * steps
    fresh = kf.shape[1]
    core = core_ref[0]
    ends = []
    for r in range(rows):
        ends.append((ends[-1] if ends else 0) + lax.div(len_ref[r] + (PAGE - 1), PAGE))
    row_of, live_of, page_of = [], [], []
    for s in range(slots):
        row, start = jnp.int32(0), jnp.int32(0)
        for r in range(rows - 1):
            past = s >= ends[r]
            row = jnp.where(past, r + 1, row)
            start = jnp.where(past, ends[r], start)
        i = s - start
        page = tab_ref[row, jnp.minimum(i, most - 1)]
        row_of.append(row)
        live_of.append(len_ref[row] - i * PAGE)
        page_of.append(page)
    kf[...] = jnp.zeros_like(kf)
    vf[...] = jnp.zeros_like(vf)
    cosv, sinv, by_row = cos[...], sin[...], scale[...]
    per = len(heads) // 2
    for i in range(len(heads)):
        src = mine if i < per else other
        at = lambda n: src[i % per, :own, n * HD : (n + 1) * HD] * by_row + bias[i : i + 1, n * HD : (n + 1) * HD]
        turn = lambda v: v * cosv + pltpu.roll(v, HD // 2, 1) * sinv
        for n in range(group):
            v = turn(at(n))
            for r in range(rows):
                q32[i, r, n * steps : (n + 1) * steps, :] = v[r * steps : (r + 1) * steps]
        kf[i, :own, :] = turn(at(group))
        vf[i, :own, :] = at(group + 1)
    qb[...] = q32[...].astype(BF)
    top[...] = jnp.full_like(top, -1e30)
    factor = 1.0 / HD**0.5
    nt = (((1,), (1,)), ((), ()))
    lane = lax.broadcasted_iota(jnp.int32, (lanes, PAGE), 1)
    flane = lax.broadcasted_iota(jnp.int32, (lanes, fresh), 1)
    fstep = lax.rem(lax.broadcasted_iota(jnp.int32, (lanes, fresh), 0), steps)
    for i in range(len(heads)):
        head = heads[i](core)
        for s in range(slots):
            row = row_of[s]
            v = lax.dot_general(qb[i, row], keys[page_of[s], head], nt, preferred_element_type=F32) * factor
            v = jnp.where(lane < live_of[s], v, -1e30)
            score[i, s] = v
            top[i, row] = jnp.maximum(top[i, row], v)
        for r in range(rows):
            v = lax.dot_general(qb[i, r], kf[i].astype(BF), nt, preferred_element_type=F32) * factor
            ok = (flane >= r * steps) & (flane - r * steps <= fstep)
            v = jnp.where(ok, v, -1e30)
            most_v = jnp.maximum(jnp.max(top[i, r], 1, keepdims=True), jnp.max(v, 1, keepdims=True))
            top[i, r] = jnp.broadcast_to(most_v, (lanes, PAGE))
            e = jnp.where(ok, jnp.exp(v - most_v), 0.0)
            low[i, r] = jnp.where(lane == 0, jnp.sum(e, 1, keepdims=True), 0.0)
            acc[i, r] = jnp.dot(e.astype(BF), vf[i].astype(BF), preferred_element_type=F32)
        for s in range(slots):
            row = row_of[s]
            e = jnp.exp(score[i, s] - top[i, row])
            low[i, row] = low[i, row] + e
            acc[i, row] = acc[i, row] + jnp.dot(e.astype(BF), vals[page_of[s], head], preferred_element_type=F32)
        for r in range(rows):
            v = (acc[i, r] / jnp.sum(low[i, r], 1, keepdims=True)).astype(BF)
            for n in range(group):
                at_col = pl.multiple_of(head * (group * HD), HD) + n * HD
                out[r, :, pl.ds(pl.multiple_of(at_col, HD), HD)] = v[n * steps : (n + 1) * steps]


def attend_paged(core, mine, other, scale, bias, cos, sin, key_pages, value_pages, kv_lengths, page_table):
    rows = kv_lengths.shape[0]
    steps = scale.shape[0] // rows
    group = HQ // KVH
    slots = key_pages.shape[0]
    per = KVH // 2
    heads = [lambda c, g=g: c + 2 * g for g in range(per)] + [lambda c, g=g: 1 - c + 2 * g for g in range(per)]
    smem = pl.BlockSpec(memory_space=pltpu.SMEM)
    vmem = pl.BlockSpec(memory_space=pltpu.VMEM)
    key_pages, value_pages = (pltpu.with_memory_space_constraint(a, pltpu.VMEM) for a in (key_pages, value_pages))
    part = (KVH, rows, group * steps, HD)
    own16 = -(-rows * steps // 16) * 16
    return pl.pallas_call(
        functools.partial(attend_kernel, heads),
        out_shape=jax.ShapeDtypeStruct((rows, steps, HQ * HD), BF),
        in_specs=[smem] * 3 + [vmem] * 8,
        out_specs=vmem,
        scratch_shapes=[
            pltpu.VMEM(part, F32),
            pltpu.VMEM(part, BF),
            pltpu.VMEM((KVH, own16, HD), F32),
            pltpu.VMEM((KVH, own16, HD), F32),
            pltpu.VMEM((KVH, slots, group * steps, PAGE), F32),
            pltpu.VMEM(part, F32),
            pltpu.VMEM(part, F32),
            pltpu.VMEM(part, F32),
        ],
        compiler_params=pltpu.CompilerParams(vmem_limit_bytes=12 << 20),
        name="attend_paged",
    )(kv_lengths, page_table, core.reshape(1), mine, other, scale, bias, cos, sin, key_pages, value_pages)


def turns(kv_lengths, steps):
    positions = kv_lengths[:, None] + jnp.arange(steps, dtype=jnp.int32)[None, :]
    half = HD // 2
    freq = THETA ** (-(jnp.arange(half, dtype=F32) * 2.0 / HD))
    angle = positions.reshape(-1).astype(F32)[:, None] * freq
    cos, sin = jnp.cos(angle), jnp.sin(angle)
    return jnp.concatenate([cos, cos], 1), jnp.concatenate([-sin, sin], 1)


def weights_plan(hidden, norm_gain, w_query, w_key, w_value, bias_query, bias_key, bias_value,
                 key_pages, value_pages, kv_lengths, page_table):
    shards = tuple(w.astype(BF) for w in (w_query, w_key, w_value))
    whole = lax.all_gather(hidden, "tp", axis=2, tiled=True)
    count, steps, width = whole.shape
    wide = whole.astype(F32)
    power = jnp.mean(wide * wide, axis=2, keepdims=True)
    normed = (wide * lax.rsqrt(power + EPS) * norm_gain).astype(BF).reshape(count * steps, width)
    made = []
    for shard, bias in zip(shards, (bias_query, bias_key, bias_value)):
        local = lax.all_to_all(shard, "tp", split_axis=1, concat_axis=0, tiled=True)
        piece = lax.all_gather(local, "replica", axis=0, tiled=True)
        total = jnp.dot(normed, piece, preferred_element_type=F32) + bias
        out = total.astype(BF).reshape(count, steps, -1)
        made.append(lax.all_to_all(out, "tp", split_axis=0, concat_axis=2, tiled=True))
    rows = made[0].shape[0]
    query = made[0].reshape(rows, steps, HQ, HD)
    key_new = made[1].reshape(rows, steps, KVH, HD)
    value_new = made[2].reshape(rows, steps, KVH, HD)
    return attend(query, key_new, value_new, key_pages, value_pages, kv_lengths, page_table)


def cast_kernel(core_ref, wq, wk, wv, own, sib):
    i = pl.program_id(0)
    per = pl.num_programs(0) // 2

    def put(out):
        qw = wq.shape[1]
        out[0, :, :qw] = wq[...].astype(BF)
        out[0, :, qw : qw + HD] = wk[...].astype(BF)
        out[0, :, qw + HD :] = wv[...].astype(BF)

    pl.when(i < per)(lambda: put(own))
    pl.when(i >= per)(lambda: put(sib))


def cast_weights(core, w_query, w_key, w_value):
    kw, qw, per = w_query.shape[0], HQ // KVH * HD, KVH // 2
    head = lambda i, c: jnp.where(i < per, c[0] + 2 * i, 1 - c[0] + 2 * (i - per))
    spec = lambda w: pl.BlockSpec((kw, w), lambda i, c: (0, head(i, c)))
    shape = jax.ShapeDtypeStruct((per, kw, qw + 2 * HD), BF)
    block = (1,) + shape.shape[1:]
    return pl.pallas_call(
        cast_kernel,
        out_shape=(shape, shape),
        grid_spec=pltpu.PrefetchScalarGridSpec(
            num_scalar_prefetch=1,
            grid=(2 * per,),
            in_specs=[spec(qw), spec(HD), spec(HD)],
            out_specs=[
                pl.BlockSpec(block, lambda i, c: (jnp.minimum(i, per - 1), 0, 0)),
                pl.BlockSpec(block, lambda i, c: (jnp.maximum(i - per, 0), 0, 0)),
            ],
        ),
        compiler_params=pltpu.CompilerParams(vmem_limit_bytes=24 << 20),
        name="cast_weights",
    )(core.reshape(1), w_query, w_key, w_value)


def after(a, *others):
    return lax.optimization_barrier((a,) + others)[0]


def sums_plan(R, T, hidden, norm_gain, w_query, w_key, w_value, bias_query, bias_key, bias_value,
              key_pages, value_pages, kv_lengths, page_table):
    ri, ti = lax.axis_index("replica"), lax.axis_index("tp")
    y, z, c, x = ri % 2, ri // 2, ti % 2, ti // 2
    zh, zl = z // 2, z % 2
    count, steps, width = hidden.shape
    kw = w_query.shape[0]
    D = norm_gain.shape[0]
    rows = count // T
    own = rows * steps
    G = KVH // 2
    gw = HQ // KVH * HD + 2 * HD

    def perm(f):
        pairs = []
        for i in range(R * T):
            r, t = divmod(i, T)
            zz, yy, xx, cc = f(r // 2, r % 2, t // 2, t % 2)
            pairs.append((i, (zz * 2 + yy) * T + xx * 2 + cc))
        return pairs

    def flip(dz=0, dy=0, dx=0, dc=0):
        return perm(lambda z, y, x, c: (z ^ dz, y ^ dy, x ^ dx, c ^ dc))

    def send(a, pairs):
        return lax.ppermute(a, AXES, pairs)

    pick = lambda a, i, axis=0: lax.dynamic_index_in_dim(a, i, axis, keepdims=False)

    gain = lax.dynamic_slice_in_dim(norm_gain, ti * width, width)
    acts = (hidden.astype(F32) * gain).astype(BF).reshape(T * own, 2, 2, 2 * kw).transpose(1, 2, 0, 3)
    start = acts
    acts = send(acts, perm(lambda z, y, x, c: (z // 2 * 2 + c, y, x, z % 2)))
    there = acts
    at = lambda dy, dx: pick(pick(acts, y ^ dy), x ^ dx)
    block = lambda dy, dx: send(at(dy, dx), flip(dy=dy, dx=dx)) if dy or dx else at(0, 0)
    acts = jnp.stack([jnp.stack([block(0, dx), block(1, dx)]) for dx in range(2)])
    far = pick(acts, 1 ^ zh ^ x)
    acts = jnp.stack([pick(acts, zh ^ x), send(far, flip(dz=2))])
    acts = jnp.stack([acts, send(acts, flip(dc=1))])

    w_own, w_sib = cast_weights(after(c, start), w_query, w_key, w_value)
    w_sib = send(after(w_sib, there), flip(dc=1))

    late = after(hidden, there).astype(F32)
    power = jnp.sum(late * late, axis=2).reshape(T * own)
    bias = jnp.concatenate([bias_query, bias_key, bias_value])
    got = send(jnp.concatenate([bias, power]), flip(dx=1))
    biases = jnp.stack([jnp.where(x == 0, bias, got[:gw]), jnp.where(x == 0, got[:gw], bias)])
    power = power + got[gw:]
    got = send(jnp.concatenate([biases.reshape(-1), power]), flip(dc=1))
    biases = jnp.concatenate([biases, got[: G * gw].reshape(G, gw)])
    power = pick((power + got[G * gw :]).reshape(T, own), ti)
    row_scale = jnp.broadcast_to(lax.rsqrt(power / D + EPS)[:, None], (own, HD))
    cos, sin = turns(after(kv_lengths, there), steps)

    def dot(a, g):
        f = lambda i, w: jnp.einsum("abymk,kn->abymn", pick(a.reshape(a.shape[:-1] + (2, kw)), i, 4), w[g],
                                    preferred_element_type=F32)
        return f(c, w_own) + f(1 - c, w_sib)

    half = lambda a, i: pick(a.reshape(a.shape[:3] + (2, 2 * own, a.shape[-1])), i, 3)
    to_x, to_y = flip(dx=1), flip(dy=1)
    parts = []
    for g in range(G):
        if g % 2 == 0:
            got = send(dot(half(acts, 1 - x), g).astype(BF), to_x)
            part = dot(half(acts, x), g) + got
            part = part[:, :, 0] + send(part[:, :, 1].astype(BF), to_y)
        else:
            got = send(dot(acts[:, :, 1:], g).astype(BF), to_y)
            part = dot(acts[:, :, :1], g) + got
            got = send(half(part, 1 - x)[:, :, 0].astype(BF), to_x)
            part = half(part, x)[:, :, 0] + got
        parts.append(part)
    parts = jnp.stack(parts, 2)
    at = lambda k: pick(parts[:, k // 2], zl ^ c ^ (k % 2))
    total = at(0)
    for k in range(1, R // 2):
        total = total + send(at(k).astype(BF), flip(dz=k))
    total = total.reshape(G, 2, own, gw)
    mine, other = pick(total, c, 1), send(pick(total, 1 - c, 1), flip(dc=1))
    return attend_paged(
        c, mine, other, row_scale, biases, cos, sin, key_pages, value_pages, kv_lengths, page_table
    )


def solution(mesh):
    R, T = mesh.shape["replica"], mesh.shape["tp"]

    def on_device(hidden, norm_gain, *rest):
        m = hidden.shape[0] * hidden.shape[1] * R
        few_rows = m * T < norm_gain.shape[0]
        two_ways = T == KVH and R == 2 * T
        if few_rows and two_ways:
            return sums_plan(R, T, hidden, norm_gain, *rest)
        return weights_plan(hidden, norm_gain, *rest)

    split = ("replica", "tp")
    in_specs = (
        P("replica", None, "tp"), P(), P(split, None), P(split, None), P(split, None),
        P("tp"), P("tp"), P("tp"),
        P(split, None, None, None), P(split, None, None, None), P(split), P(split, None),
    )
    return jax.shard_map(
        on_device, mesh=mesh, in_specs=in_specs, out_specs=P(split, None, None), check_vma=False
    )
```
